32 devices in a mesh: groups: 2 (over y), seq: 4 (over z), dp: 2 (over x), mp: 2 (over core).
Axes of the slice: x: 2, y: 2, z: 4, core: 2. Of those that a mesh axis runs over, the one named last changes fastest.
Arguments:
- queries: bfloat16 [4, 512, 2048], P(('groups', 'dp'), 'seq', 'mp'), parts along dimension 0, may hold values from -6 to 6
- keys: bfloat16 [4, 512, 2048], P(('groups', 'dp'), 'seq', 'mp'), parts along dimension 0, may hold values from -6 to 6
- values: bfloat16 [4, 512, 2048], P(('groups', 'dp'), 'seq', 'mp'), parts along dimension 0, may hold values from -6 to 6
- grad_output: bfloat16 [4, 512, 2048], P(('groups', 'dp'), 'seq', 'mp'), parts along dimension 0, may hold values from -6 to 6
- counts: int32 [4, 4, 4], P(('groups', 'dp'), 'seq'), parts along dimension 0, may hold values from 0 to 64, as said below
Outputs:
- grad_queries: bfloat16 [4, 512, 2048], P(('groups', 'dp'), 'seq', 'mp'), parts along dimension 0
- grad_keys: bfloat16 [4, 512, 2048], P(('groups', 'dp'), 'seq', 'mp'), parts along dimension 0
- grad_values: bfloat16 [4, 512, 2048], P(('groups', 'dp'), 'seq', 'mp'), parts along dimension 0
The draws below stay inside these ranges and needn't reach their ends.
There are 2 independent parts, one for each index of `groups`. The reference program is written for one: setup_inputs(seed, part) draws one part's arguments, and reference() takes and returns one part's arrays. A program takes and returns all parts, laid end to end along the dimension named above; each array names one. Nothing has to cross between parts.
Inputs may be any that keep to these rules, and one draw needn't show every extreme that they name: Each shard's counts sum to 128; no entry exceeds 64, some window receives 64 points from every shard.
All inputs are finite; a program needn't handle non-finite values.
Results may differ from the reference program's by a relative error of at most 0.001.
Values may be sent and summed in bfloat16 or wider, within the bound.
A program may use at most 128 MiB of HBM per device.

```python
import math
import jax
import jax.numpy as jnp
from jax import lax

HEADS = 16
DH = 128
R_SRC = 128
WIDTH = 2048
SLOT = 64
ROWS = 512
STREAMS = 2
N_SEQ = 4


def draw_counts(key, part):
    mean_count = R_SRC // N_SEQ
    half_seq = N_SEQ // 2
    first_key, second_key, third_key = jax.random.split(jax.random.fold_in(key, 7), 3)
    base = jax.random.randint(first_key, (STREAMS, 1, half_seq), 0, 2 * mean_count + 1)
    spread = jax.random.randint(second_key, (STREAMS, N_SEQ, half_seq), -(mean_count // 2), mean_count // 2 + 1)
    forced = jax.random.randint(third_key, (STREAMS, 1, 1), 0, half_seq)
    pair_index = jnp.arange(half_seq, dtype=jnp.int32)[None, None, :]
    first_half = jnp.clip(base + spread, 0, 2 * mean_count)
    first_half = jnp.where(pair_index == forced, 2 * mean_count, first_half)
    paired = jnp.stack([first_half, 2 * mean_count - first_half], axis=-1)
    return paired.reshape(STREAMS, N_SEQ, N_SEQ).astype(jnp.int32)


def level_of(rng, extent, cuts, least, top_value):
    level, own = 1.0, jax.random.fold_in(rng, 6)
    for dim, parts in cuts:
        steps = jnp.exp(jax.random.uniform(jax.random.fold_in(own, dim), (parts,), jnp.float32, least / len(cuts), top_value / len(cuts)))
        level = level * jnp.repeat(steps, extent[dim] // parts).reshape([-1 if axis == dim else 1 for axis in range(len(extent))])
    return level


def bell_draw(rng, dims, scale, limit, shards=(), held_as=jnp.bfloat16):
    drawn = scale * jax.random.normal(rng, dims, jnp.float32)
    if shards:
        drawn = drawn * level_of(rng, dims, shards, -0.22, 0.18)
    return jnp.clip(drawn, -limit, limit).astype(held_as)


def setup_inputs(seed: int = 0, part: int = 0) -> dict:
    key_of = jax.random.split(jax.random.key(seed), 6)
    part_keys = jax.random.split(jax.random.fold_in(key_of[5], part), 6)
    queries = bell_draw(part_keys[0], (STREAMS, ROWS, WIDTH), 1.0, 6.0, ((0, 2), (1, 4), (2, 2)))
    keys = bell_draw(part_keys[1], (STREAMS, ROWS, WIDTH), 1.0, 6.0, ((0, 2), (1, 4), (2, 2)))
    values = bell_draw(part_keys[2], (STREAMS, ROWS, WIDTH), 1.0, 6.0, ((0, 2), (1, 4), (2, 2)))
    grad_output = bell_draw(part_keys[3], (STREAMS, ROWS, WIDTH), 1.0, 6.0, ((0, 2), (1, 4), (2, 2)))
    counts = draw_counts(jax.random.fold_in(jax.random.fold_in(key_of[5], part), 71), part)
    return dict(queries=queries, keys=keys, values=values, grad_output=grad_output, counts=counts)


highest = lax.Precision.HIGHEST

def window_index(stream_counts):
    shard_starts = jnp.cumsum(stream_counts, axis=1) - stream_counts
    slot_offsets = jnp.arange(SLOT, dtype=jnp.int32)
    shard_base = jnp.arange(N_SEQ, dtype=jnp.int32) * R_SRC
    source_rows = shard_base[None, :, None] + shard_starts.T[:, :, None] + slot_offsets[None, None, :]
    occupied = slot_offsets[None, None, :] < stream_counts.T[:, :, None]
    return (source_rows.reshape(-1).astype(jnp.int32), occupied.reshape(-1))

def head_gradients(query_seq, key_seq, value_seq, grad_seq):
    total = query_seq.shape[0]
    block = 128 if total % 128 == 0 else total
    nblocks = total // block
    lower = (lax.broadcasted_iota(jnp.int32, (block, block), 0) >= lax.broadcasted_iota(jnp.int32, (block, block), 1)).astype(jnp.float32)
    pieces = tuple((x.reshape(nblocks, block, DH) for x in (query_seq, key_seq, value_seq, grad_seq)))

    def forward_step(state, part):
        query_b, key_b, value_b, grad_b = part
        weights = jnp.dot(grad_b, value_b.T, precision=highest) * lower
        grad_q = jnp.dot(grad_b, state.T, precision=highest) + jnp.dot(weights, key_b, precision=highest)
        state = state + jnp.dot(key_b.T, value_b, precision=highest)
        return (state, grad_q)

    def reverse_step(state, part):
        query_b, key_b, value_b, grad_b = part
        weights = jnp.dot(grad_b, value_b.T, precision=highest) * lower
        scores = jnp.dot(query_b, key_b.T, precision=highest) * lower
        grad_k = jnp.dot(value_b, state.T, precision=highest) + jnp.dot(weights.T, query_b, precision=highest)
        grad_v = jnp.dot(key_b, state, precision=highest) + jnp.dot(scores.T, grad_b, precision=highest)
        state = state + jnp.dot(query_b.T, grad_b, precision=highest)
        return (state, (grad_k, grad_v))
    start = jnp.zeros((DH, DH), jnp.float32)
    _, grad_q = lax.scan(forward_step, start, pieces)
    _, (grad_k, grad_v) = lax.scan(reverse_step, start, pieces, reverse=True)
    return (grad_q.reshape(total, DH), grad_k.reshape(total, DH), grad_v.reshape(total, DH))

def stream_gradients(operands):
    query_rows, key_rows, value_rows, grad_rows, stream_counts = operands
    factor = 1.0 / math.sqrt(DH * ROWS)
    source_rows, occupied = window_index(stream_counts)
    picked = jnp.where(occupied, source_rows, 0).astype(jnp.int32)

    def arrange(source):
        gathered = jnp.take(source, picked, axis=0).astype(jnp.float32)
        gathered = jnp.where(occupied[:, None], gathered, jnp.zeros_like(gathered))
        return gathered.reshape(-1, HEADS, DH).transpose(1, 0, 2)
    grad_q, grad_k, grad_v = jax.vmap(head_gradients)(arrange(query_rows), arrange(key_rows), arrange(value_rows), arrange(grad_rows))
    target = jnp.where(occupied, source_rows, ROWS).astype(jnp.int32)

    def place(result):
        flat_result = (result.transpose(1, 0, 2).reshape(-1, HEADS * DH) * factor).astype(jnp.bfloat16)
        return jnp.zeros((ROWS, HEADS * DH), jnp.bfloat16).at[target].set(flat_result, mode='drop')
    return (place(grad_q), place(grad_k), place(grad_v))

def reference(queries, keys, values, grad_output, counts):
    grad_queries, grad_keys, grad_values = lax.map(stream_gradients, (queries, keys, values, grad_output, counts))
    return (grad_queries, grad_keys, grad_values)
```

```python
import functools
import math

import jax
import jax.numpy as jnp
from jax import lax
from jax.experimental import pallas as pl
from jax.experimental.pallas import tpu as pltpu
from jax.sharding import PartitionSpec as P

DH = 128


highest = lax.Precision.HIGHEST


def entering(value, axis, join, neutral, backward):
    count, mine = (lax.axis_size(axis), lax.axis_index(axis))
    pieces = lax.all_gather(value, axis)
    if backward:
        pieces = pieces[::-1]
        mine = count - 1 - mine
    total = jnp.full_like(value, 0) + jnp.asarray(neutral, value.dtype)

    def hop(position, total):
        longer = join(total, pieces[position])
        return jnp.where(position < mine, longer, total)

    return lax.fori_loop(0, count - 1, hop, total)


def add_states(earlier, later):
    return earlier + later


def per_device(queries, keys, values, grad_output, counts):
    shard_count = lax.axis_size("seq")
    local_rows = queries.shape[1]
    width = queries.shape[2]
    local_heads = width // DH
    capacity = 2 * local_rows // shard_count
    window_rows = shard_count * capacity
    factor = 1.0 / math.sqrt(DH * local_rows * shard_count)
    my_counts = counts[0, 0]
    window_ends = jnp.cumsum(my_counts)
    window_starts = window_ends - my_counts
    offsets = jnp.arange(capacity, dtype=jnp.int32)
    occupied = offsets[None, :] < my_counts[:, None]
    picked = jnp.where(occupied, window_starts[:, None] + offsets[None, :], 0).reshape(-1)
    occupied_column = occupied.reshape(-1, 1)

    def pack(source):
        taken = jnp.take(source[0], picked, axis=0)
        taken = jnp.where(occupied_column, taken, jnp.zeros_like(taken))
        return taken.reshape(shard_count, capacity, width)

    def split_heads(received):
        return received.reshape(window_rows, local_heads, DH)

    def outer_sum(left, right):
        return jnp.einsum("lha,lhb->hab", left, right, preferred_element_type=jnp.float32)

    query_recv, key_recv, value_recv, grad_recv = (
        lax.all_to_all(pack(queries), "seq", split_axis=0, concat_axis=0, tiled=True),
        lax.all_to_all(pack(keys), "seq", split_axis=0, concat_axis=0, tiled=True),
        lax.all_to_all(pack(values), "seq", split_axis=0, concat_axis=0, tiled=True),
        lax.all_to_all(pack(grad_output), "seq", split_axis=0, concat_axis=0, tiled=True),
    )
    query_recv = split_heads(query_recv)
    key_recv = split_heads(key_recv)
    value_recv = split_heads(value_recv)
    grad_recv = split_heads(grad_recv)
    key_state = outer_sum(key_recv, value_recv)
    query_state = outer_sum(query_recv, grad_recv)
    zero_state = jnp.zeros((local_heads, DH, DH), jnp.float32)
    before_kv = entering(key_state, "seq", add_states, zero_state, False)
    after_qd = entering(query_state, "seq", add_states, zero_state, True)
    block = min(512, window_rows)
    nblocks = window_rows // block

    def blocked(received):
        return received.reshape(nblocks, block, local_heads, DH)

    query_blocks = blocked(query_recv)
    key_blocks = blocked(key_recv)
    value_blocks = blocked(value_recv)
    grad_blocks = blocked(grad_recv)
    block_kv = jnp.einsum(
        "nlha,nlhb->nhab", key_blocks, value_blocks, preferred_element_type=jnp.float32
    )
    block_qd = jnp.einsum(
        "nlha,nlhb->nhab", query_blocks, grad_blocks, preferred_element_type=jnp.float32
    )
    kv_before = before_kv[None] + jnp.cumsum(block_kv, axis=0) - block_kv
    qd_after = after_qd[None] + jnp.sum(block_qd, axis=0)[None] - jnp.cumsum(block_qd, axis=0)
    lower = (
        lax.broadcasted_iota(jnp.int32, (block, block), 0)
        >= lax.broadcasted_iota(jnp.int32, (block, block), 1)
    ).astype(jnp.float32)

    def one_block(pieces):
        query_part, key_part, value_part, grad_part, kv_state, qd_state = pieces
        weights = (
            jnp.einsum("rha,sha->hrs", grad_part, value_part, preferred_element_type=jnp.float32)
            * lower[None]
        )
        scores = (
            jnp.einsum("rha,sha->hrs", query_part, key_part, preferred_element_type=jnp.float32)
            * lower[None]
        )
        query_f = query_part.astype(jnp.float32)
        key_f = key_part.astype(jnp.float32)
        value_f = value_part.astype(jnp.float32)
        grad_f = grad_part.astype(jnp.float32)
        grad_q = jnp.einsum("rhb,hab->rha", grad_f, kv_state, precision=highest) + jnp.einsum(
            "hrs,sha->rha", weights, key_f, precision=highest
        )
        grad_k = jnp.einsum("shb,hab->sha", value_f, qd_state, precision=highest) + jnp.einsum(
            "hrs,rha->sha", weights, query_f, precision=highest
        )
        grad_v = jnp.einsum("sha,hab->shb", key_f, qd_state, precision=highest) + jnp.einsum(
            "hrs,rhb->shb", scores, grad_f, precision=highest
        )

        def finish(result):
            return (result * factor).astype(jnp.bfloat16).reshape(block, width)

        return (finish(grad_q), finish(grad_k), finish(grad_v))

    out_q, out_k, out_v = lax.map(
        one_block, (query_blocks, key_blocks, value_blocks, grad_blocks, kv_before, qd_after)
    )

    def to_slots(result):
        return result.reshape(shard_count, capacity, width)

    back_q, back_k, back_v = (
        lax.all_to_all(to_slots(out_q), "seq", split_axis=0, concat_axis=0, tiled=True),
        lax.all_to_all(to_slots(out_k), "seq", split_axis=0, concat_axis=0, tiled=True),
        lax.all_to_all(to_slots(out_v), "seq", split_axis=0, concat_axis=0, tiled=True),
    )
    positions = jnp.arange(local_rows, dtype=jnp.int32)
    member = (
        (positions[:, None] >= window_starts[None, :]) & (positions[:, None] < window_ends[None, :])
    ).astype(jnp.int32)
    window_of = jnp.sum(member * jnp.arange(shard_count, dtype=jnp.int32)[None, :], axis=1)
    start_of = jnp.sum(member * window_starts[None, :], axis=1)
    source_index = window_of * capacity + positions - start_of

    def unpack(returned):
        return jnp.take(returned.reshape(window_rows, width), source_index, axis=0)[None]

    return (unpack(back_q), unpack(back_k), unpack(back_v))


MESH = pl.DeviceIdType.MESH


def exchange_kernel(
    n,
    rows,
    owned,
    q_ref,
    k_ref,
    v_ref,
    g_ref,
    counts_ref,
    dq_ref,
    dk_ref,
    dv_ref,
    held,
    ends,
    key_row,
    key_col,
    result,
    in_send,
    in_recv,
    own_sem,
    ends_send,
    ends_recv,
    out_send,
    out_recv,
    back_sem,
):
    me = lax.axis_index("seq")
    total = n * rows
    factor = 1.0 / math.sqrt(DH * total)
    sources = (q_ref, k_ref, v_ref, g_ref)
    outputs = (dq_ref, dk_ref, dv_ref)
    peers = [lax.rem(me + d, n) for d in range(n)]
    senders = [lax.rem(me + n - d, n) for d in range(n)]

    def columns(owner, head):
        return pl.ds(pl.multiple_of((owner * owned + head) * DH, DH), DH)

    def block(shard):
        return pl.ds(pl.multiple_of(shard * rows, rows), rows)

    barrier = pltpu.get_barrier_semaphore()
    for d in range(1, n):
        pl.semaphore_signal(barrier, inc=1, device_id={"seq": peers[d]}, device_id_type=MESH)

    own = [
        [
            pltpu.make_async_copy(
                sources[t].at[0, :, columns(me, h)], held.at[h, t, block(me)], own_sem.at[h, t]
            )
            for t in range(4)
        ]
        for h in range(owned)
    ]
    for h in range(owned):
        for t in range(4):
            own[h][t].start()

    lanes = lax.broadcasted_iota(jnp.int32, (8, 128), 1)
    end = jnp.zeros((1, 1), jnp.int32)
    table = jnp.zeros((8, 128), jnp.int32)
    for w in range(n):
        end = end + counts_ref[0, 0:1, w : w + 1]
        table = jnp.where(lanes == w, end, table)
    ends[me] = table

    pl.semaphore_wait(barrier, n - 1)

    ends_copies = [None]
    for d in range(1, n):
        copy = pltpu.make_async_remote_copy(
            src_ref=ends.at[me],
            dst_ref=ends.at[me],
            send_sem=ends_send.at[d],
            recv_sem=ends_recv.at[d],
            device_id={"seq": peers[d]},
            device_id_type=MESH,
        )
        copy.start()
        ends_copies.append(copy)

    in_copies = {}
    for h in range(owned):
        for t in range(4):
            for d in range(1, n):
                copy = pltpu.make_async_remote_copy(
                    src_ref=sources[t].at[0, :, columns(peers[d], h)],
                    dst_ref=held.at[h, t, block(me)],
                    send_sem=in_send.at[h, t, d],
                    recv_sem=in_recv.at[h, t, d],
                    device_id={"seq": peers[d]},
                    device_id_type=MESH,
                )
                copy.start()
                in_copies[h, t, d] = copy

    def arrive(h, t, d):
        return pltpu.make_async_remote_copy(
            src_ref=sources[t].at[0, :, columns(me, h)],
            dst_ref=held.at[h, t, block(senders[d])],
            send_sem=in_send.at[h, t, d],
            recv_sem=in_recv.at[h, t, d],
            device_id={"seq": peers[d]},
            device_id_type=MESH,
        )

    for d in range(1, n):
        pltpu.make_async_remote_copy(
            src_ref=ends.at[me],
            dst_ref=ends.at[senders[d]],
            send_sem=ends_send.at[d],
            recv_sem=ends_recv.at[d],
            device_id={"seq": peers[d]},
            device_id_type=MESH,
        ).wait_recv()

    across = lax.broadcasted_iota(jnp.int32, (1, rows), 1)
    down = lax.broadcasted_iota(jnp.int32, (rows, 128), 0)
    for s in range(n):
        window_row = jnp.zeros((1, rows), jnp.int32)
        window_col = jnp.zeros((rows, 128), jnp.int32)
        for w in range(n):
            stop = ends[s, 0:1, w : w + 1]
            window_row = window_row + jnp.where(across >= stop, 1, 0)
            window_col = window_col + jnp.where(down >= stop, 1, 0)
        key_row[0:1, s * rows : (s + 1) * rows] = (window_row * n + s) * rows + across
        key_col[s] = (window_col * n + s) * rows + down

    def scores(left, right):
        return lax.dot_general(
            left, right, (((1,), (1,)), ((), ())), preferred_element_type=jnp.float32
        )

    def weighted(weights, right):
        high = weights.astype(jnp.bfloat16)
        low = (weights - high.astype(jnp.float32)).astype(jnp.bfloat16)
        product = jnp.dot(high, right, preferred_element_type=jnp.float32) + jnp.dot(
            low, right, preferred_element_type=jnp.float32
        )
        return (product * factor).astype(jnp.bfloat16)

    back_copies = []
    for h in range(owned):
        for t in range(4):
            own[h][t].wait()
            for d in range(1, n):
                arrive(h, t, d).wait_recv()
        for step in range(1, n + 1):
            d = step % n
            s = peers[d]
            col = jnp.concatenate([key_col[s]] * (total // 128), axis=1)
            row = key_row[...]
            earlier = row <= col
            later = row >= col
            q_all, k_all = (held[h, 0], held[h, 1])
            v_all, g_all = (held[h, 2], held[h, 3])
            k_own, v_own = (held[h, 1, block(s), :], held[h, 2, block(s), :])
            g_own = held[h, 3, block(s), :]
            result[h, 0, s] = weighted(jnp.where(earlier, scores(g_own, v_all), 0.0), k_all)
            result[h, 1, s] = weighted(jnp.where(later, scores(v_own, g_all), 0.0), q_all)
            result[h, 2, s] = weighted(jnp.where(later, scores(k_own, q_all), 0.0), g_all)
            for t in range(3):
                if d == 0:
                    copy = pltpu.make_async_copy(
                        result.at[h, t, s], outputs[t].at[0, :, columns(me, h)], back_sem.at[h, t]
                    )
                else:
                    copy = pltpu.make_async_remote_copy(
                        src_ref=result.at[h, t, s],
                        dst_ref=outputs[t].at[0, :, columns(me, h)],
                        send_sem=out_send.at[h, t, d],
                        recv_sem=out_recv.at[h, t, d],
                        device_id={"seq": s},
                        device_id_type=MESH,
                    )
                copy.start()
                back_copies.append((d, copy))

    for d in range(1, n):
        ends_copies[d].wait_send()
    for copy in in_copies.values():
        copy.wait_send()
    for h in range(owned):
        for d in range(1, n):
            for t in range(3):
                pltpu.make_async_remote_copy(
                    src_ref=result.at[h, t, me],
                    dst_ref=outputs[t].at[0, :, columns(senders[d], h)],
                    send_sem=out_send.at[h, t, d],
                    recv_sem=out_recv.at[h, t, d],
                    device_id={"seq": peers[d]},
                    device_id_type=MESH,
                ).wait_recv()
    for d, copy in back_copies:
        if d == 0:
            copy.wait()
        else:
            copy.wait_send()


def by_heads(queries, keys, values, grad_output, counts):
    n = lax.axis_size("seq")
    rows, width = queries.shape[1:]
    owned = width // DH // n
    dma = pltpu.SemaphoreType.DMA
    anywhere = pl.BlockSpec(memory_space=pl.ANY)
    return pl.pallas_call(
        functools.partial(exchange_kernel, n, rows, owned),
        out_shape=[jax.ShapeDtypeStruct(queries.shape, jnp.bfloat16)] * 3,
        in_specs=[anywhere] * 4 + [pl.BlockSpec(memory_space=pltpu.VMEM)],
        out_specs=[anywhere] * 3,
        scratch_shapes=[
            pltpu.VMEM((owned, 4, n * rows, DH), jnp.bfloat16),
            pltpu.VMEM((n, 8, 128), jnp.int32),
            pltpu.VMEM((1, n * rows), jnp.int32),
            pltpu.VMEM((n, rows, 128), jnp.int32),
            pltpu.VMEM((owned, 3, n, rows, DH), jnp.bfloat16),
            dma((owned, 4, n)),
            dma((owned, 4, n)),
            dma((owned, 4)),
            dma((n,)),
            dma((n,)),
            dma((owned, 3, n)),
            dma((owned, 3, n)),
            dma((owned, 3)),
        ],
        compiler_params=pltpu.CompilerParams(collective_id=0, has_side_effects=True),
    )(queries, keys, values, grad_output, counts)


def per_shard(queries, keys, values, grad_output, counts):
    n = lax.axis_size("seq")
    rows, width = queries.shape[1:]
    heads = width // DH
    if heads % n == 0 and rows % 128 == 0 and n <= 128:
        return by_heads(queries, keys, values, grad_output, counts)
    return per_device(queries, keys, values, grad_output, counts)


def solution(mesh):
    placed = (
        P(("groups", "dp"), "seq", "mp"),
        P(("groups", "dp"), "seq", "mp"),
        P(("groups", "dp"), "seq", "mp"),
        P(("groups", "dp"), "seq", "mp"),
        P(("groups", "dp"), "seq", None),
    )
    return jax.shard_map(
        per_shard,
        mesh=mesh,
        in_specs=placed,
        out_specs=(
            P(("groups", "dp"), "seq", "mp"),
            P(("groups", "dp"), "seq", "mp"),
            P(("groups", "dp"), "seq", "mp"),
        ),
        check_vma=False,
    )
```

```python
import functools
import math

import jax
import jax.numpy as jnp
from jax import lax
from jax.experimental import pallas as pl
from jax.experimental.pallas import tpu as pltpu
from jax.sharding import PartitionSpec as P

DH = 128


highest = lax.Precision.HIGHEST


def entering(value, axis, join, neutral, backward):
    count, mine = (lax.axis_size(axis), lax.axis_index(axis))
    pieces = lax.all_gather(value, axis)
    if backward:
        pieces = pieces[::-1]
        mine = count - 1 - mine
    total = jnp.full_like(value, 0) + jnp.asarray(neutral, value.dtype)

    def hop(position, total):
        longer = join(total, pieces[position])
        return jnp.where(position < mine, longer, total)

    return lax.fori_loop(0, count - 1, hop, total)


def add_states(earlier, later):
    return earlier + later


def per_device(queries, keys, values, grad_output, counts):
    shard_count = lax.axis_size("seq")
    local_rows = queries.shape[1]
    width = queries.shape[2]
    local_heads = width // DH
    capacity = 2 * local_rows // shard_count
    window_rows = shard_count * capacity
    factor = 1.0 / math.sqrt(DH * local_rows * shard_count)
    my_counts = counts[0, 0]
    window_ends = jnp.cumsum(my_counts)
    window_starts = window_ends - my_counts
    offsets = jnp.arange(capacity, dtype=jnp.int32)
    occupied = offsets[None, :] < my_counts[:, None]
    picked = jnp.where(occupied, window_starts[:, None] + offsets[None, :], 0).reshape(-1)
    occupied_column = occupied.reshape(-1, 1)

    def pack(source):
        taken = jnp.take(source[0], picked, axis=0)
        taken = jnp.where(occupied_column, taken, jnp.zeros_like(taken))
        return taken.reshape(shard_count, capacity, width)

    def split_heads(received):
        return received.reshape(window_rows, local_heads, DH)

    def outer_sum(left, right):
        return jnp.einsum("lha,lhb->hab", left, right, preferred_element_type=jnp.float32)

    query_recv, key_recv, value_recv, grad_recv = (
        lax.all_to_all(pack(queries), "seq", split_axis=0, concat_axis=0, tiled=True),
        lax.all_to_all(pack(keys), "seq", split_axis=0, concat_axis=0, tiled=True),
        lax.all_to_all(pack(values), "seq", split_axis=0, concat_axis=0, tiled=True),
        lax.all_to_all(pack(grad_output), "seq", split_axis=0, concat_axis=0, tiled=True),
    )
    query_recv = split_heads(query_recv)
    key_recv = split_heads(key_recv)
    value_recv = split_heads(value_recv)
    grad_recv = split_heads(grad_recv)
    key_state = outer_sum(key_recv, value_recv)
    query_state = outer_sum(query_recv, grad_recv)
    zero_state = jnp.zeros((local_heads, DH, DH), jnp.float32)
    before_kv = entering(key_state, "seq", add_states, zero_state, False)
    after_qd = entering(query_state, "seq", add_states, zero_state, True)
    block = min(512, window_rows)
    nblocks = window_rows // block

    def blocked(received):
        return received.reshape(nblocks, block, local_heads, DH)

    query_blocks = blocked(query_recv)
    key_blocks = blocked(key_recv)
    value_blocks = blocked(value_recv)
    grad_blocks = blocked(grad_recv)
    block_kv = jnp.einsum(
        "nlha,nlhb->nhab", key_blocks, value_blocks, preferred_element_type=jnp.float32
    )
    block_qd = jnp.einsum(
        "nlha,nlhb->nhab", query_blocks, grad_blocks, preferred_element_type=jnp.float32
    )
    kv_before = before_kv[None] + jnp.cumsum(block_kv, axis=0) - block_kv
    qd_after = after_qd[None] + jnp.sum(block_qd, axis=0)[None] - jnp.cumsum(block_qd, axis=0)
    lower = (
        lax.broadcasted_iota(jnp.int32, (block, block), 0)
        >= lax.broadcasted_iota(jnp.int32, (block, block), 1)
    ).astype(jnp.float32)

    def one_block(pieces):
        query_part, key_part, value_part, grad_part, kv_state, qd_state = pieces
        weights = (
            jnp.einsum("rha,sha->hrs", grad_part, value_part, preferred_element_type=jnp.float32)
            * lower[None]
        )
        scores = (
            jnp.einsum("rha,sha->hrs", query_part, key_part, preferred_element_type=jnp.float32)
            * lower[None]
        )
        query_f = query_part.astype(jnp.float32)
        key_f = key_part.astype(jnp.float32)
        value_f = value_part.astype(jnp.float32)
        grad_f = grad_part.astype(jnp.float32)
        grad_q = jnp.einsum("rhb,hab->rha", grad_f, kv_state, precision=highest) + jnp.einsum(
            "hrs,sha->rha", weights, key_f, precision=highest
        )
        grad_k = jnp.einsum("shb,hab->sha", value_f, qd_state, precision=highest) + jnp.einsum(
            "hrs,rha->sha", weights, query_f, precision=highest
        )
        grad_v = jnp.einsum("sha,hab->shb", key_f, qd_state, precision=highest) + jnp.einsum(
            "hrs,rhb->shb", scores, grad_f, precision=highest
        )

        def finish(result):
            return (result * factor).astype(jnp.bfloat16).reshape(block, width)

        return (finish(grad_q), finish(grad_k), finish(grad_v))

    out_q, out_k, out_v = lax.map(
        one_block, (query_blocks, key_blocks, value_blocks, grad_blocks, kv_before, qd_after)
    )

    def to_slots(result):
        return result.reshape(shard_count, capacity, width)

    back_q, back_k, back_v = (
        lax.all_to_all(to_slots(out_q), "seq", split_axis=0, concat_axis=0, tiled=True),
        lax.all_to_all(to_slots(out_k), "seq", split_axis=0, concat_axis=0, tiled=True),
        lax.all_to_all(to_slots(out_v), "seq", split_axis=0, concat_axis=0, tiled=True),
    )
    positions = jnp.arange(local_rows, dtype=jnp.int32)
    member = (
        (positions[:, None] >= window_starts[None, :]) & (positions[:, None] < window_ends[None, :])
    ).astype(jnp.int32)
    window_of = jnp.sum(member * jnp.arange(shard_count, dtype=jnp.int32)[None, :], axis=1)
    start_of = jnp.sum(member * window_starts[None, :], axis=1)
    source_index = window_of * capacity + positions - start_of

    def unpack(returned):
        return jnp.take(returned.reshape(window_rows, width), source_index, axis=0)[None]

    return (unpack(back_q), unpack(back_k), unpack(back_v))


MESH = pl.DeviceIdType.MESH
VMEM_LIMIT = 16 << 20


def exchange_kernel(
    n,
    rows,
    owned,
    q_ref,
    k_ref,
    v_ref,
    g_ref,
    counts_ref,
    dq_ref,
    dk_ref,
    dv_ref,
    held,
    mine,
    ends,
    key_row,
    key_col,
    result,
    in_send,
    in_recv,
    own_sem,
    mine_sem,
    ends_send,
    ends_recv,
    out_send,
    out_recv,
    back_sem,
):
    me = lax.axis_index("seq")
    total = n * rows
    factor = 1.0 / math.sqrt(DH * total)
    sources = (q_ref, k_ref, v_ref, g_ref)
    outputs = (dq_ref, dk_ref, dv_ref)
    peers = [lax.rem(me + d, n) for d in range(n)]
    senders = [lax.rem(me + n - d, n) for d in range(n)]

    def columns(owner, head):
        return pl.ds(pl.multiple_of((owner * owned + head) * DH, DH), DH)

    def block(shard):
        return pl.ds(pl.multiple_of(shard * rows, rows), rows)

    barrier = pltpu.get_barrier_semaphore()
    for d in range(1, n):
        pl.semaphore_signal(barrier, inc=1, device_id={"seq": peers[d]}, device_id_type=MESH)

    load = pltpu.make_async_copy(counts_ref, mine, mine_sem)
    load.start()
    own = [
        [
            pltpu.make_async_copy(
                sources[t].at[0, :, columns(me, h)], held.at[h, t, block(me)], own_sem.at[h, t]
            )
            for t in range(4)
        ]
        for h in range(owned)
    ]
    for h in range(owned):
        for t in range(4):
            own[h][t].start()

    load.wait()
    lanes = lax.broadcasted_iota(jnp.int32, (8, 128), 1)
    end = jnp.zeros((1, 1), jnp.int32)
    table = jnp.zeros((8, 128), jnp.int32)
    for w in range(n):
        end = end + mine[0, 0:1, w : w + 1]
        table = jnp.where(lanes == w, end, table)
    ends[me] = table

    pl.semaphore_wait(barrier, n - 1)

    ends_copies = [None]
    for d in range(1, n):
        copy = pltpu.make_async_remote_copy(
            src_ref=ends.at[me],
            dst_ref=ends.at[me],
            send_sem=ends_send.at[d],
            recv_sem=ends_recv.at[d],
            device_id={"seq": peers[d]},
            device_id_type=MESH,
        )
        copy.start()
        ends_copies.append(copy)

    in_copies = {}
    for h in range(owned):
        for t in range(4):
            for d in range(1, n):
                copy = pltpu.make_async_remote_copy(
                    src_ref=sources[t].at[0, :, columns(peers[d], h)],
                    dst_ref=held.at[h, t, block(me)],
                    send_sem=in_send.at[h, t, d],
                    recv_sem=in_recv.at[h, t, d],
                    device_id={"seq": peers[d]},
                    device_id_type=MESH,
                )
                copy.start()
                in_copies[h, t, d] = copy

    def arrive(h, t, d):
        return pltpu.make_async_remote_copy(
            src_ref=sources[t].at[0, :, columns(me, h)],
            dst_ref=held.at[h, t, block(senders[d])],
            send_sem=in_send.at[h, t, d],
            recv_sem=in_recv.at[h, t, d],
            device_id={"seq": peers[d]},
            device_id_type=MESH,
        )

    for d in range(1, n):
        pltpu.make_async_remote_copy(
            src_ref=ends.at[me],
            dst_ref=ends.at[senders[d]],
            send_sem=ends_send.at[d],
            recv_sem=ends_recv.at[d],
            device_id={"seq": peers[d]},
            device_id_type=MESH,
        ).wait_recv()

    across = lax.broadcasted_iota(jnp.int32, (1, rows), 1)
    down = lax.broadcasted_iota(jnp.int32, (rows, 128), 0)
    for s in range(n):
        window_row = jnp.zeros((1, rows), jnp.int32)
        window_col = jnp.zeros((rows, 128), jnp.int32)
        for w in range(n):
            stop = ends[s, 0:1, w : w + 1]
            window_row = window_row + jnp.where(across >= stop, 1, 0)
            window_col = window_col + jnp.where(down >= stop, 1, 0)
        key_row[0:1, s * rows : (s + 1) * rows] = (window_row * n + s) * rows + across
        key_col[s] = (window_col * n + s) * rows + down

    def scores(left, right):
        return lax.dot_general(
            left, right, (((1,), (1,)), ((), ())), preferred_element_type=jnp.float32
        )

    def weighted(weights, right):
        high = weights.astype(jnp.bfloat16)
        low = (weights - high.astype(jnp.float32)).astype(jnp.bfloat16)
        product = jnp.dot(high, right, preferred_element_type=jnp.float32) + jnp.dot(
            low, right, preferred_element_type=jnp.float32
        )
        return (product * factor).astype(jnp.bfloat16)

    back_copies = []
    for h in range(owned):
        for t in range(4):
            own[h][t].wait()
            for d in range(1, n):
                arrive(h, t, d).wait_recv()
        for step in range(1, n + 1):
            d = step % n
            s = peers[d]
            col = jnp.concatenate([key_col[s]] * (total // 128), axis=1)
            row = key_row[...]
            earlier = row <= col
            later = row >= col
            q_all, k_all = (held[h, 0], held[h, 1])
            v_all, g_all = (held[h, 2], held[h, 3])
            k_own, v_own = (held[h, 1, block(s), :], held[h, 2, block(s), :])
            g_own = held[h, 3, block(s), :]
            result[h, 0, s] = weighted(jnp.where(earlier, scores(g_own, v_all), 0.0), k_all)
            result[h, 1, s] = weighted(jnp.where(later, scores(v_own, g_all), 0.0), q_all)
            result[h, 2, s] = weighted(jnp.where(later, scores(k_own, q_all), 0.0), g_all)
            for t in range(3):
                if d == 0:
                    copy = pltpu.make_async_copy(
                        result.at[h, t, s], outputs[t].at[0, :, columns(me, h)], back_sem.at[h, t]
                    )
                else:
                    copy = pltpu.make_async_remote_copy(
                        src_ref=result.at[h, t, s],
                        dst_ref=outputs[t].at[0, :, columns(me, h)],
                        send_sem=out_send.at[h, t, d],
                        recv_sem=out_recv.at[h, t, d],
                        device_id={"seq": s},
                        device_id_type=MESH,
                    )
                copy.start()
                back_copies.append((d, copy))

    for d in range(1, n):
        ends_copies[d].wait_send()
    for copy in in_copies.values():
        copy.wait_send()
    for h in range(owned):
        for d in range(1, n):
            for t in range(3):
                pltpu.make_async_remote_copy(
                    src_ref=result.at[h, t, me],
                    dst_ref=outputs[t].at[0, :, columns(senders[d], h)],
                    send_sem=out_send.at[h, t, d],
                    recv_sem=out_recv.at[h, t, d],
                    device_id={"seq": peers[d]},
                    device_id_type=MESH,
                ).wait_recv()
    for d, copy in back_copies:
        if d == 0:
            copy.wait()
        else:
            copy.wait_send()


def place_kernel(a_ref, b_ref, c_ref, x_ref, y_ref, z_ref, sem):
    copies = [
        pltpu.make_async_copy(source, target, sem.at[i])
        for i, (source, target) in enumerate(((a_ref, x_ref), (b_ref, y_ref), (c_ref, z_ref)))
    ]
    for copy in copies:
        copy.start()
    for copy in copies:
        copy.wait()


def by_heads(queries, keys, values, grad_output, counts):
    n = lax.axis_size("seq")
    rows, width = queries.shape[1:]
    owned = width // DH // n
    dma = pltpu.SemaphoreType.DMA
    anywhere = pl.BlockSpec(memory_space=pl.ANY)
    shapes = [jax.ShapeDtypeStruct(queries.shape, jnp.bfloat16)] * 3
    gradients = pl.pallas_call(
        functools.partial(exchange_kernel, n, rows, owned),
        out_shape=shapes,
        in_specs=[pl.BlockSpec(memory_space=pltpu.HBM)] * 5,
        out_specs=[anywhere] * 3,
        scratch_shapes=[
            pltpu.VMEM((owned, 4, n * rows, DH), jnp.bfloat16),
            pltpu.VMEM((1, 1, n), jnp.int32),
            pltpu.VMEM((n, 8, 128), jnp.int32),
            pltpu.VMEM((1, n * rows), jnp.int32),
            pltpu.VMEM((n, rows, 128), jnp.int32),
            pltpu.VMEM((owned, 3, n, rows, DH), jnp.bfloat16),
            dma((owned, 4, n)),
            dma((owned, 4, n)),
            dma((owned, 4)),
            dma(()),
            dma((n,)),
            dma((n,)),
            dma((owned, 3, n)),
            dma((owned, 3, n)),
            dma((owned, 3)),
        ],
        compiler_params=pltpu.CompilerParams(collective_id=0, has_side_effects=True, vmem_limit_bytes=VMEM_LIMIT),
    )(*(pltpu.with_memory_space_constraint(x, pltpu.HBM) for x in (queries, keys, values, grad_output, counts)))
    return pl.pallas_call(
        place_kernel,
        out_shape=shapes,
        in_specs=[anywhere] * 3,
        out_specs=[anywhere] * 3,
        scratch_shapes=[dma((3,))],
        compiler_params=pltpu.CompilerParams(vmem_limit_bytes=VMEM_LIMIT),
    )(*gradients)


def per_shard(queries, keys, values, grad_output, counts):
    n = lax.axis_size("seq")
    rows, width = queries.shape[1:]
    heads = width // DH
    if heads % n == 0 and rows % 128 == 0 and n <= 128:
        return by_heads(queries, keys, values, grad_output, counts)
    return per_device(queries, keys, values, grad_output, counts)


def solution(mesh):
    placed = (
        P(("groups", "dp"), "seq", "mp"),
        P(("groups", "dp"), "seq", "mp"),
        P(("groups", "dp"), "seq", "mp"),
        P(("groups", "dp"), "seq", "mp"),
        P(("groups", "dp"), "seq", None),
    )
    return jax.shard_map(
        per_shard,
        mesh=mesh,
        in_specs=placed,
        out_specs=(
            P(("groups", "dp"), "seq", "mp"),
            P(("groups", "dp"), "seq", "mp"),
            P(("groups", "dp"), "seq", "mp"),
        ),
        check_vma=False,
    )
```

```python
import functools
import math

import jax
import jax.numpy as jnp
from jax import lax
from jax.experimental import pallas as pl
from jax.experimental.pallas import tpu as pltpu
from jax.sharding import PartitionSpec as P

DH = 128


highest = lax.Precision.HIGHEST


def entering(value, axis, join, neutral, backward):
    count, mine = (lax.axis_size(axis), lax.axis_index(axis))
    pieces = lax.all_gather(value, axis)
    if backward:
        pieces = pieces[::-1]
        mine = count - 1 - mine
    total = jnp.full_like(value, 0) + jnp.asarray(neutral, value.dtype)

    def hop(position, total):
        longer = join(total, pieces[position])
        return jnp.where(position < mine, longer, total)

    return lax.fori_loop(0, count - 1, hop, total)


def add_states(earlier, later):
    return earlier + later


def per_device(queries, keys, values, grad_output, counts):
    shard_count = lax.axis_size("seq")
    local_rows = queries.shape[1]
    width = queries.shape[2]
    local_heads = width // DH
    capacity = 2 * local_rows // shard_count
    window_rows = shard_count * capacity
    factor = 1.0 / math.sqrt(DH * local_rows * shard_count)
    my_counts = counts[0, 0]
    window_ends = jnp.cumsum(my_counts)
    window_starts = window_ends - my_counts
    offsets = jnp.arange(capacity, dtype=jnp.int32)
    occupied = offsets[None, :] < my_counts[:, None]
    picked = jnp.where(occupied, window_starts[:, None] + offsets[None, :], 0).reshape(-1)
    occupied_column = occupied.reshape(-1, 1)

    def pack(source):
        taken = jnp.take(source[0], picked, axis=0)
        taken = jnp.where(occupied_column, taken, jnp.zeros_like(taken))
        return taken.reshape(shard_count, capacity, width)

    def split_heads(received):
        return received.reshape(window_rows, local_heads, DH)

    def outer_sum(left, right):
        return jnp.einsum("lha,lhb->hab", left, right, preferred_element_type=jnp.float32)

    query_recv, key_recv, value_recv, grad_recv = (
        lax.all_to_all(pack(queries), "seq", split_axis=0, concat_axis=0, tiled=True),
        lax.all_to_all(pack(keys), "seq", split_axis=0, concat_axis=0, tiled=True),
        lax.all_to_all(pack(values), "seq", split_axis=0, concat_axis=0, tiled=True),
        lax.all_to_all(pack(grad_output), "seq", split_axis=0, concat_axis=0, tiled=True),
    )
    query_recv = split_heads(query_recv)
    key_recv = split_heads(key_recv)
    value_recv = split_heads(value_recv)
    grad_recv = split_heads(grad_recv)
    key_state = outer_sum(key_recv, value_recv)
    query_state = outer_sum(query_recv, grad_recv)
    zero_state = jnp.zeros((local_heads, DH, DH), jnp.float32)
    before_kv = entering(key_state, "seq", add_states, zero_state, False)
    after_qd = entering(query_state, "seq", add_states, zero_state, True)
    block = min(512, window_rows)
    nblocks = window_rows // block

    def blocked(received):
        return received.reshape(nblocks, block, local_heads, DH)

    query_blocks = blocked(query_recv)
    key_blocks = blocked(key_recv)
    value_blocks = blocked(value_recv)
    grad_blocks = blocked(grad_recv)
    block_kv = jnp.einsum(
        "nlha,nlhb->nhab", key_blocks, value_blocks, preferred_element_type=jnp.float32
    )
    block_qd = jnp.einsum(
        "nlha,nlhb->nhab", query_blocks, grad_blocks, preferred_element_type=jnp.float32
    )
    kv_before = before_kv[None] + jnp.cumsum(block_kv, axis=0) - block_kv
    qd_after = after_qd[None] + jnp.sum(block_qd, axis=0)[None] - jnp.cumsum(block_qd, axis=0)
    lower = (
        lax.broadcasted_iota(jnp.int32, (block, block), 0)
        >= lax.broadcasted_iota(jnp.int32, (block, block), 1)
    ).astype(jnp.float32)

    def one_block(pieces):
        query_part, key_part, value_part, grad_part, kv_state, qd_state = pieces
        weights = (
            jnp.einsum("rha,sha->hrs", grad_part, value_part, preferred_element_type=jnp.float32)
            * lower[None]
        )
        scores = (
            jnp.einsum("rha,sha->hrs", query_part, key_part, preferred_element_type=jnp.float32)
            * lower[None]
        )
        query_f = query_part.astype(jnp.float32)
        key_f = key_part.astype(jnp.float32)
        value_f = value_part.astype(jnp.float32)
        grad_f = grad_part.astype(jnp.float32)
        grad_q = jnp.einsum("rhb,hab->rha", grad_f, kv_state, precision=highest) + jnp.einsum(
            "hrs,sha->rha", weights, key_f, precision=highest
        )
        grad_k = jnp.einsum("shb,hab->sha", value_f, qd_state, precision=highest) + jnp.einsum(
            "hrs,rha->sha", weights, query_f, precision=highest
        )
        grad_v = jnp.einsum("sha,hab->shb", key_f, qd_state, precision=highest) + jnp.einsum(
            "hrs,rhb->shb", scores, grad_f, precision=highest
        )

        def finish(result):
            return (result * factor).astype(jnp.bfloat16).reshape(block, width)

        return (finish(grad_q), finish(grad_k), finish(grad_v))

    out_q, out_k, out_v = lax.map(
        one_block, (query_blocks, key_blocks, value_blocks, grad_blocks, kv_before, qd_after)
    )

    def to_slots(result):
        return result.reshape(shard_count, capacity, width)

    back_q, back_k, back_v = (
        lax.all_to_all(to_slots(out_q), "seq", split_axis=0, concat_axis=0, tiled=True),
        lax.all_to_all(to_slots(out_k), "seq", split_axis=0, concat_axis=0, tiled=True),
        lax.all_to_all(to_slots(out_v), "seq", split_axis=0, concat_axis=0, tiled=True),
    )
    positions = jnp.arange(local_rows, dtype=jnp.int32)
    member = (
        (positions[:, None] >= window_starts[None, :]) & (positions[:, None] < window_ends[None, :])
    ).astype(jnp.int32)
    window_of = jnp.sum(member * jnp.arange(shard_count, dtype=jnp.int32)[None, :], axis=1)
    start_of = jnp.sum(member * window_starts[None, :], axis=1)
    source_index = window_of * capacity + positions - start_of

    def unpack(returned):
        return jnp.take(returned.reshape(window_rows, width), source_index, axis=0)[None]

    return (unpack(back_q), unpack(back_k), unpack(back_v))


MESH = pl.DeviceIdType.MESH
VMEM_LIMIT = 16 << 20


def exchange_kernel(
    n,
    rows,
    owned,
    q_ref,
    k_ref,
    v_ref,
    g_ref,
    counts_ref,
    dq_ref,
    dk_ref,
    dv_ref,
    held,
    mine,
    ends,
    key_row,
    key_col,
    result,
    in_send,
    in_recv,
    own_sem,
    mine_sem,
    ends_send,
    ends_recv,
    out_send,
    out_recv,
    back_sem,
):
    me = lax.axis_index("seq")
    total = n * rows
    factor = 1.0 / math.sqrt(DH * total)
    sources = (q_ref, k_ref, v_ref, g_ref)
    outputs = (dq_ref, dk_ref, dv_ref)
    peers = [lax.rem(me + d, n) for d in range(n)]
    order = sorted(range(1, n), key=lambda d: abs(d - n // 2))
    senders = [lax.rem(me + n - d, n) for d in range(n)]

    def columns(owner, head):
        return pl.ds(pl.multiple_of((owner * owned + head) * DH, DH), DH)

    def block(shard):
        return pl.ds(pl.multiple_of(shard * rows, rows), rows)

    barrier = pltpu.get_barrier_semaphore()
    for d in range(1, n):
        pl.semaphore_signal(barrier, inc=1, device_id={"seq": peers[d]}, device_id_type=MESH)

    load = pltpu.make_async_copy(counts_ref, mine, mine_sem)
    load.start()
    own = [
        [
            pltpu.make_async_copy(
                sources[t].at[0, :, columns(me, h)], held.at[h, t, block(me)], own_sem.at[h, t]
            )
            for t in range(4)
        ]
        for h in range(owned)
    ]
    for h in range(owned):
        for t in range(4):
            own[h][t].start()

    load.wait()
    lanes = lax.broadcasted_iota(jnp.int32, (8, 128), 1)
    end = jnp.zeros((1, 1), jnp.int32)
    table = jnp.zeros((8, 128), jnp.int32)
    for w in range(n):
        end = end + mine[0, 0:1, w : w + 1]
        table = jnp.where(lanes == w, end, table)
    ends[me] = table

    pl.semaphore_wait(barrier, n - 1)

    ends_copies = [None]
    for d in range(1, n):
        copy = pltpu.make_async_remote_copy(
            src_ref=ends.at[me],
            dst_ref=ends.at[me],
            send_sem=ends_send.at[d],
            recv_sem=ends_recv.at[d],
            device_id={"seq": peers[d]},
            device_id_type=MESH,
        )
        copy.start()
        ends_copies.append(copy)

    in_copies = {}
    for h in range(owned):
        for t in range(4):
            for d in order:
                copy = pltpu.make_async_remote_copy(
                    src_ref=sources[t].at[0, :, columns(peers[d], h)],
                    dst_ref=held.at[h, t, block(me)],
                    send_sem=in_send.at[h, t, d],
                    recv_sem=in_recv.at[h, t, d],
                    device_id={"seq": peers[d]},
                    device_id_type=MESH,
                )
                copy.start()
                in_copies[h, t, d] = copy

    def arrive(h, t, d):
        return pltpu.make_async_remote_copy(
            src_ref=sources[t].at[0, :, columns(me, h)],
            dst_ref=held.at[h, t, block(senders[d])],
            send_sem=in_send.at[h, t, d],
            recv_sem=in_recv.at[h, t, d],
            device_id={"seq": peers[d]},
            device_id_type=MESH,
        )

    for d in range(1, n):
        pltpu.make_async_remote_copy(
            src_ref=ends.at[me],
            dst_ref=ends.at[senders[d]],
            send_sem=ends_send.at[d],
            recv_sem=ends_recv.at[d],
            device_id={"seq": peers[d]},
            device_id_type=MESH,
        ).wait_recv()

    across = lax.broadcasted_iota(jnp.int32, (1, rows), 1)
    down = lax.broadcasted_iota(jnp.int32, (rows, 128), 0)
    for s in range(n):
        window_row = jnp.zeros((1, rows), jnp.int32)
        window_col = jnp.zeros((rows, 128), jnp.int32)
        for w in range(n):
            stop = ends[s, 0:1, w : w + 1]
            window_row = window_row + jnp.where(across >= stop, 1, 0)
            window_col = window_col + jnp.where(down >= stop, 1, 0)
        key_row[0:1, s * rows : (s + 1) * rows] = (window_row * n + s) * rows + across
        key_col[s] = (window_col * n + s) * rows + down

    def scores(left, right):
        return lax.dot_general(
            left, right, (((1,), (1,)), ((), ())), preferred_element_type=jnp.float32
        )

    def weighted(weights, right):
        high = weights.astype(jnp.bfloat16)
        low = (weights - high.astype(jnp.float32)).astype(jnp.bfloat16)
        product = jnp.dot(high, right, preferred_element_type=jnp.float32) + jnp.dot(
            low, right, preferred_element_type=jnp.float32
        )
        return (product * factor).astype(jnp.bfloat16)

    back_copies = []

    def give(h, t, d, s):
        if d == 0:
            copy = pltpu.make_async_copy(
                result.at[h, t, s], outputs[t].at[0, :, columns(me, h)], back_sem.at[h, t]
            )
        else:
            copy = pltpu.make_async_remote_copy(
                src_ref=result.at[h, t, s],
                dst_ref=outputs[t].at[0, :, columns(me, h)],
                send_sem=out_send.at[h, t, d],
                recv_sem=out_recv.at[h, t, d],
                device_id={"seq": s},
                device_id_type=MESH,
            )
        copy.start()
        back_copies.append((d, copy))

    for h in range(owned):
        for t in range(4):
            own[h][t].wait()
            for d in range(1, n):
                arrive(h, t, d).wait_recv()
        for d in order + [0]:
            s = peers[d]
            col = jnp.concatenate([key_col[s]] * (total // 128), axis=1)
            row = key_row[...]
            earlier = row <= col
            later = row >= col
            q_all, k_all = (held[h, 0], held[h, 1])
            v_all, g_all = (held[h, 2], held[h, 3])
            k_own, v_own = (held[h, 1, block(s), :], held[h, 2, block(s), :])
            g_own = held[h, 3, block(s), :]
            result[h, 0, s] = weighted(jnp.where(earlier, scores(g_own, v_all), 0.0), k_all)
            give(h, 0, d, s)
            result[h, 1, s] = weighted(jnp.where(later, scores(v_own, g_all), 0.0), q_all)
            give(h, 1, d, s)
            result[h, 2, s] = weighted(jnp.where(later, scores(k_own, q_all), 0.0), g_all)
            give(h, 2, d, s)

    for d in range(1, n):
        ends_copies[d].wait_send()
    for copy in in_copies.values():
        copy.wait_send()
    for h in range(owned):
        for d in range(1, n):
            for t in range(3):
                pltpu.make_async_remote_copy(
                    src_ref=result.at[h, t, me],
                    dst_ref=outputs[t].at[0, :, columns(senders[d], h)],
                    send_sem=out_send.at[h, t, d],
                    recv_sem=out_recv.at[h, t, d],
                    device_id={"seq": peers[d]},
                    device_id_type=MESH,
                ).wait_recv()
    for d, copy in back_copies:
        if d == 0:
            copy.wait()
        else:
            copy.wait_send()


def place_kernel(a_ref, b_ref, c_ref, x_ref, y_ref, z_ref, sem):
    copies = [
        pltpu.make_async_copy(source, target, sem.at[i])
        for i, (source, target) in enumerate(((a_ref, x_ref), (b_ref, y_ref), (c_ref, z_ref)))
    ]
    for copy in copies:
        copy.start()
    for copy in copies:
        copy.wait()


def by_heads(queries, keys, values, grad_output, counts):
    n = lax.axis_size("seq")
    rows, width = queries.shape[1:]
    owned = width // DH // n
    dma = pltpu.SemaphoreType.DMA
    anywhere = pl.BlockSpec(memory_space=pl.ANY)
    shapes = [jax.ShapeDtypeStruct(queries.shape, jnp.bfloat16)] * 3
    gradients = pl.pallas_call(
        functools.partial(exchange_kernel, n, rows, owned),
        out_shape=shapes,
        in_specs=[pl.BlockSpec(memory_space=pltpu.HBM)] * 5,
        out_specs=[anywhere] * 3,
        scratch_shapes=[
            pltpu.VMEM((owned, 4, n * rows, DH), jnp.bfloat16),
            pltpu.VMEM((1, 1, n), jnp.int32),
            pltpu.VMEM((n, 8, 128), jnp.int32),
            pltpu.VMEM((1, n * rows), jnp.int32),
            pltpu.VMEM((n, rows, 128), jnp.int32),
            pltpu.VMEM((owned, 3, n, rows, DH), jnp.bfloat16),
            dma((owned, 4, n)),
            dma((owned, 4, n)),
            dma((owned, 4)),
            dma(()),
            dma((n,)),
            dma((n,)),
            dma((owned, 3, n)),
            dma((owned, 3, n)),
            dma((owned, 3)),
        ],
        compiler_params=pltpu.CompilerParams(collective_id=0, has_side_effects=True, vmem_limit_bytes=VMEM_LIMIT),
    )(*(pltpu.with_memory_space_constraint(x, pltpu.HBM) for x in (queries, keys, values, grad_output, counts)))
    return pl.pallas_call(
        place_kernel,
        out_shape=shapes,
        in_specs=[anywhere] * 3,
        out_specs=[anywhere] * 3,
        scratch_shapes=[dma((3,))],
        compiler_params=pltpu.CompilerParams(vmem_limit_bytes=VMEM_LIMIT),
    )(*gradients)


def per_shard(queries, keys, values, grad_output, counts):
    n = lax.axis_size("seq")
    rows, width = queries.shape[1:]
    heads = width // DH
    if heads % n == 0 and rows % 128 == 0 and n <= 128:
        return by_heads(queries, keys, values, grad_output, counts)
    return per_device(queries, keys, values, grad_output, counts)


def solution(mesh):
    placed = (
        P(("groups", "dp"), "seq", "mp"),
        P(("groups", "dp"), "seq", "mp"),
        P(("groups", "dp"), "seq", "mp"),
        P(("groups", "dp"), "seq", "mp"),
        P(("groups", "dp"), "seq", None),
    )
    return jax.shard_map(
        per_shard,
        mesh=mesh,
        in_specs=placed,
        out_specs=(
            P(("groups", "dp"), "seq", "mp"),
            P(("groups", "dp"), "seq", "mp"),
            P(("groups", "dp"), "seq", "mp"),
        ),
        check_vma=False,
    )
```

```python
import functools
import math

import jax
import jax.numpy as jnp
from jax import lax
from jax.experimental import pallas as pl
from jax.experimental.pallas import tpu as pltpu
from jax.sharding import PartitionSpec as P

DH = 128


highest = lax.Precision.HIGHEST


def entering(value, axis, join, neutral, backward):
    count, mine = (lax.axis_size(axis), lax.axis_index(axis))
    pieces = lax.all_gather(value, axis)
    if backward:
        pieces = pieces[::-1]
        mine = count - 1 - mine
    total = jnp.full_like(value, 0) + jnp.asarray(neutral, value.dtype)

    def hop(position, total):
        longer = join(total, pieces[position])
        return jnp.where(position < mine, longer, total)

    return lax.fori_loop(0, count - 1, hop, total)


def add_states(earlier, later):
    return earlier + later


def per_device(queries, keys, values, grad_output, counts):
    shard_count = lax.axis_size("seq")
    local_rows = queries.shape[1]
    width = queries.shape[2]
    local_heads = width // DH
    capacity = 2 * local_rows // shard_count
    window_rows = shard_count * capacity
    factor = 1.0 / math.sqrt(DH * local_rows * shard_count)
    my_counts = counts[0, 0]
    window_ends = jnp.cumsum(my_counts)
    window_starts = window_ends - my_counts
    offsets = jnp.arange(capacity, dtype=jnp.int32)
    occupied = offsets[None, :] < my_counts[:, None]
    picked = jnp.where(occupied, window_starts[:, None] + offsets[None, :], 0).reshape(-1)
    occupied_column = occupied.reshape(-1, 1)

    def pack(source):
        taken = jnp.take(source[0], picked, axis=0)
        taken = jnp.where(occupied_column, taken, jnp.zeros_like(taken))
        return taken.reshape(shard_count, capacity, width)

    def split_heads(received):
        return received.reshape(window_rows, local_heads, DH)

    def outer_sum(left, right):
        return jnp.einsum("lha,lhb->hab", left, right, preferred_element_type=jnp.float32)

    query_recv, key_recv, value_recv, grad_recv = (
        lax.all_to_all(pack(queries), "seq", split_axis=0, concat_axis=0, tiled=True),
        lax.all_to_all(pack(keys), "seq", split_axis=0, concat_axis=0, tiled=True),
        lax.all_to_all(pack(values), "seq", split_axis=0, concat_axis=0, tiled=True),
        lax.all_to_all(pack(grad_output), "seq", split_axis=0, concat_axis=0, tiled=True),
    )
    query_recv = split_heads(query_recv)
    key_recv = split_heads(key_recv)
    value_recv = split_heads(value_recv)
    grad_recv = split_heads(grad_recv)
    key_state = outer_sum(key_recv, value_recv)
    query_state = outer_sum(query_recv, grad_recv)
    zero_state = jnp.zeros((local_heads, DH, DH), jnp.float32)
    before_kv = entering(key_state, "seq", add_states, zero_state, False)
    after_qd = entering(query_state, "seq", add_states, zero_state, True)
    block = min(512, window_rows)
    nblocks = window_rows // block

    def blocked(received):
        return received.reshape(nblocks, block, local_heads, DH)

    query_blocks = blocked(query_recv)
    key_blocks = blocked(key_recv)
    value_blocks = blocked(value_recv)
    grad_blocks = blocked(grad_recv)
    block_kv = jnp.einsum(
        "nlha,nlhb->nhab", key_blocks, value_blocks, preferred_element_type=jnp.float32
    )
    block_qd = jnp.einsum(
        "nlha,nlhb->nhab", query_blocks, grad_blocks, preferred_element_type=jnp.float32
    )
    kv_before = before_kv[None] + jnp.cumsum(block_kv, axis=0) - block_kv
    qd_after = after_qd[None] + jnp.sum(block_qd, axis=0)[None] - jnp.cumsum(block_qd, axis=0)
    lower = (
        lax.broadcasted_iota(jnp.int32, (block, block), 0)
        >= lax.broadcasted_iota(jnp.int32, (block, block), 1)
    ).astype(jnp.float32)

    def one_block(pieces):
        query_part, key_part, value_part, grad_part, kv_state, qd_state = pieces
        weights = (
            jnp.einsum("rha,sha->hrs", grad_part, value_part, preferred_element_type=jnp.float32)
            * lower[None]
        )
        scores = (
            jnp.einsum("rha,sha->hrs", query_part, key_part, preferred_element_type=jnp.float32)
            * lower[None]
        )
        query_f = query_part.astype(jnp.float32)
        key_f = key_part.astype(jnp.float32)
        value_f = value_part.astype(jnp.float32)
        grad_f = grad_part.astype(jnp.float32)
        grad_q = jnp.einsum("rhb,hab->rha", grad_f, kv_state, precision=highest) + jnp.einsum(
            "hrs,sha->rha", weights, key_f, precision=highest
        )
        grad_k = jnp.einsum("shb,hab->sha", value_f, qd_state, precision=highest) + jnp.einsum(
            "hrs,rha->sha", weights, query_f, precision=highest
        )
        grad_v = jnp.einsum("sha,hab->shb", key_f, qd_state, precision=highest) + jnp.einsum(
            "hrs,rhb->shb", scores, grad_f, precision=highest
        )

        def finish(result):
            return (result * factor).astype(jnp.bfloat16).reshape(block, width)

        return (finish(grad_q), finish(grad_k), finish(grad_v))

    out_q, out_k, out_v = lax.map(
        one_block, (query_blocks, key_blocks, value_blocks, grad_blocks, kv_before, qd_after)
    )

    def to_slots(result):
        return result.reshape(shard_count, capacity, width)

    back_q, back_k, back_v = (
        lax.all_to_all(to_slots(out_q), "seq", split_axis=0, concat_axis=0, tiled=True),
        lax.all_to_all(to_slots(out_k), "seq", split_axis=0, concat_axis=0, tiled=True),
        lax.all_to_all(to_slots(out_v), "seq", split_axis=0, concat_axis=0, tiled=True),
    )
    positions = jnp.arange(local_rows, dtype=jnp.int32)
    member = (
        (positions[:, None] >= window_starts[None, :]) & (positions[:, None] < window_ends[None, :])
    ).astype(jnp.int32)
    window_of = jnp.sum(member * jnp.arange(shard_count, dtype=jnp.int32)[None, :], axis=1)
    start_of = jnp.sum(member * window_starts[None, :], axis=1)
    source_index = window_of * capacity + positions - start_of

    def unpack(returned):
        return jnp.take(returned.reshape(window_rows, width), source_index, axis=0)[None]

    return (unpack(back_q), unpack(back_k), unpack(back_v))


MESH = pl.DeviceIdType.MESH
VMEM_LIMIT = 16 << 20


def exchange_kernel(
    n,
    rows,
    owned,
    q_ref,
    k_ref,
    v_ref,
    g_ref,
    counts_ref,
    dq_ref,
    dk_ref,
    dv_ref,
    held,
    mine,
    ends,
    key_row,
    key_col,
    result,
    in_send,
    in_recv,
    own_sem,
    mine_sem,
    ends_send,
    ends_recv,
    out_send,
    out_recv,
    back_sem,
):
    me = lax.axis_index("seq")
    total = n * rows
    factor = 1.0 / math.sqrt(DH * total)
    sources = (q_ref, k_ref, v_ref, g_ref)
    outputs = (dq_ref, dk_ref, dv_ref)
    peers = [lax.rem(me + d, n) for d in range(n)]
    senders = [lax.rem(me + n - d, n) for d in range(n)]

    def columns(owner, head):
        return pl.ds(pl.multiple_of((owner * owned + head) * DH, DH), DH)

    def block(shard):
        return pl.ds(pl.multiple_of(shard * rows, rows), rows)

    barrier = pltpu.get_barrier_semaphore()
    for d in range(1, n):
        pl.semaphore_signal(barrier, inc=1, device_id={"seq": peers[d]}, device_id_type=MESH)

    load = pltpu.make_async_copy(counts_ref, mine, mine_sem)
    load.start()
    own = [
        [
            pltpu.make_async_copy(
                sources[t].at[0, :, columns(me, h)], held.at[h, t, block(me)], own_sem.at[h, t]
            )
            for t in range(4)
        ]
        for h in range(owned)
    ]
    for h in range(owned):
        for t in range(4):
            own[h][t].start()

    pl.semaphore_wait(barrier, n - 1)

    in_copies = {}

    def send_head(h):
        for t in range(4):
            for d in range(1, n):
                copy = pltpu.make_async_remote_copy(
                    src_ref=sources[t].at[0, :, columns(peers[d], h)],
                    dst_ref=held.at[h, t, block(me)],
                    send_sem=in_send.at[h, t, d],
                    recv_sem=in_recv.at[h, t, d],
                    device_id={"seq": peers[d]},
                    device_id_type=MESH,
                )
                copy.start()
                in_copies[h, t, d] = copy

    send_head(0)
    load.wait()
    lanes = lax.broadcasted_iota(jnp.int32, (8, 128), 1)
    end = jnp.zeros((1, 1), jnp.int32)
    table = jnp.zeros((8, 128), jnp.int32)
    for w in range(n):
        end = end + mine[0, 0:1, w : w + 1]
        table = jnp.where(lanes == w, end, table)
    ends[me] = table

    ends_copies = [None]
    for d in range(1, n):
        copy = pltpu.make_async_remote_copy(
            src_ref=ends.at[me],
            dst_ref=ends.at[me],
            send_sem=ends_send.at[d],
            recv_sem=ends_recv.at[d],
            device_id={"seq": peers[d]},
            device_id_type=MESH,
        )
        copy.start()
        ends_copies.append(copy)

    for h in range(1, owned):
        send_head(h)

    def arrive(h, t, d):
        return pltpu.make_async_remote_copy(
            src_ref=sources[t].at[0, :, columns(me, h)],
            dst_ref=held.at[h, t, block(senders[d])],
            send_sem=in_send.at[h, t, d],
            recv_sem=in_recv.at[h, t, d],
            device_id={"seq": peers[d]},
            device_id_type=MESH,
        )

    for d in range(1, n):
        pltpu.make_async_remote_copy(
            src_ref=ends.at[me],
            dst_ref=ends.at[senders[d]],
            send_sem=ends_send.at[d],
            recv_sem=ends_recv.at[d],
            device_id={"seq": peers[d]},
            device_id_type=MESH,
        ).wait_recv()

    across = lax.broadcasted_iota(jnp.int32, (1, rows), 1)
    down = lax.broadcasted_iota(jnp.int32, (rows, 128), 0)
    for s in range(n):
        window_row = jnp.zeros((1, rows), jnp.int32)
        window_col = jnp.zeros((rows, 128), jnp.int32)
        for w in range(n):
            stop = ends[s, 0:1, w : w + 1]
            window_row = window_row + jnp.where(across >= stop, 1, 0)
            window_col = window_col + jnp.where(down >= stop, 1, 0)
        key_row[0:1, s * rows : (s + 1) * rows] = (window_row * n + s) * rows + across
        key_col[s] = (window_col * n + s) * rows + down

    def scores(left, right):
        return lax.dot_general(
            left, right, (((1,), (1,)), ((), ())), preferred_element_type=jnp.float32
        )

    def weighted(weights, right):
        high = weights.astype(jnp.bfloat16)
        low = (weights - high.astype(jnp.float32)).astype(jnp.bfloat16)
        product = jnp.dot(high, right, preferred_element_type=jnp.float32) + jnp.dot(
            low, right, preferred_element_type=jnp.float32
        )
        return (product * factor).astype(jnp.bfloat16)

    back_copies = []
    for h in range(owned):
        for t in range(4):
            own[h][t].wait()
            for d in range(1, n):
                arrive(h, t, d).wait_recv()
        for step in range(1, n + 1):
            d = step % n
            s = peers[d]
            col = jnp.concatenate([key_col[s]] * (total // 128), axis=1)
            row = key_row[...]
            earlier = row <= col
            later = row >= col
            q_all, k_all = (held[h, 0], held[h, 1])
            v_all, g_all = (held[h, 2], held[h, 3])
            k_own, v_own = (held[h, 1, block(s), :], held[h, 2, block(s), :])
            g_own = held[h, 3, block(s), :]
            result[h, 0, s] = weighted(jnp.where(earlier, scores(g_own, v_all), 0.0), k_all)
            result[h, 1, s] = weighted(jnp.where(later, scores(v_own, g_all), 0.0), q_all)
            result[h, 2, s] = weighted(jnp.where(later, scores(k_own, q_all), 0.0), g_all)
            for t in range(3):
                if d == 0:
                    copy = pltpu.make_async_copy(
                        result.at[h, t, s], outputs[t].at[0, :, columns(me, h)], back_sem.at[h, t]
                    )
                else:
                    copy = pltpu.make_async_remote_copy(
                        src_ref=result.at[h, t, s],
                        dst_ref=outputs[t].at[0, :, columns(me, h)],
                        send_sem=out_send.at[h, t, d],
                        recv_sem=out_recv.at[h, t, d],
                        device_id={"seq": s},
                        device_id_type=MESH,
                    )
                copy.start()
                back_copies.append((d, copy))

    for d in range(1, n):
        ends_copies[d].wait_send()
    for copy in in_copies.values():
        copy.wait_send()
    for h in range(owned):
        for d in range(1, n):
            for t in range(3):
                pltpu.make_async_remote_copy(
                    src_ref=result.at[h, t, me],
                    dst_ref=outputs[t].at[0, :, columns(senders[d], h)],
                    send_sem=out_send.at[h, t, d],
                    recv_sem=out_recv.at[h, t, d],
                    device_id={"seq": peers[d]},
                    device_id_type=MESH,
                ).wait_recv()
    for d, copy in back_copies:
        if d == 0:
            copy.wait()
        else:
            copy.wait_send()


def place_kernel(a_ref, b_ref, c_ref, x_ref, y_ref, z_ref, sem):
    copies = [
        pltpu.make_async_copy(source, target, sem.at[i])
        for i, (source, target) in enumerate(((a_ref, x_ref), (b_ref, y_ref), (c_ref, z_ref)))
    ]
    for copy in copies:
        copy.start()
    for copy in copies:
        copy.wait()


def by_heads(queries, keys, values, grad_output, counts):
    n = lax.axis_size("seq")
    rows, width = queries.shape[1:]
    owned = width // DH // n
    dma = pltpu.SemaphoreType.DMA
    anywhere = pl.BlockSpec(memory_space=pl.ANY)
    shapes = [jax.ShapeDtypeStruct(queries.shape, jnp.bfloat16)] * 3
    gradients = pl.pallas_call(
        functools.partial(exchange_kernel, n, rows, owned),
        out_shape=shapes,
        in_specs=[pl.BlockSpec(memory_space=pltpu.HBM)] * 5,
        out_specs=[anywhere] * 3,
        scratch_shapes=[
            pltpu.VMEM((owned, 4, n * rows, DH), jnp.bfloat16),
            pltpu.VMEM((1, 1, n), jnp.int32),
            pltpu.VMEM((n, 8, 128), jnp.int32),
            pltpu.VMEM((1, n * rows), jnp.int32),
            pltpu.VMEM((n, rows, 128), jnp.int32),
            pltpu.VMEM((owned, 3, n, rows, DH), jnp.bfloat16),
            dma((owned, 4, n)),
            dma((owned, 4, n)),
            dma((owned, 4)),
            dma(()),
            dma((n,)),
            dma((n,)),
            dma((owned, 3, n)),
            dma((owned, 3, n)),
            dma((owned, 3)),
        ],
        compiler_params=pltpu.CompilerParams(collective_id=0, has_side_effects=True, vmem_limit_bytes=VMEM_LIMIT),
    )(*(pltpu.with_memory_space_constraint(x, pltpu.HBM) for x in (queries, keys, values, grad_output, counts)))
    return pl.pallas_call(
        place_kernel,
        out_shape=shapes,
        in_specs=[anywhere] * 3,
        out_specs=[anywhere] * 3,
        scratch_shapes=[dma((3,))],
        compiler_params=pltpu.CompilerParams(vmem_limit_bytes=VMEM_LIMIT),
    )(*gradients)


def per_shard(queries, keys, values, grad_output, counts):
    n = lax.axis_size("seq")
    rows, width = queries.shape[1:]
    heads = width // DH
    if heads % n == 0 and rows % 128 == 0 and n <= 128:
        return by_heads(queries, keys, values, grad_output, counts)
    return per_device(queries, keys, values, grad_output, counts)


def solution(mesh):
    placed = (
        P(("groups", "dp"), "seq", "mp"),
        P(("groups", "dp"), "seq", "mp"),
        P(("groups", "dp"), "seq", "mp"),
        P(("groups", "dp"), "seq", "mp"),
        P(("groups", "dp"), "seq", None),
    )
    return jax.shard_map(
        per_shard,
        mesh=mesh,
        in_specs=placed,
        out_specs=(
            P(("groups", "dp"), "seq", "mp"),
            P(("groups", "dp"), "seq", "mp"),
            P(("groups", "dp"), "seq", "mp"),
        ),
        check_vma=False,
    )
```
